32 devices in a mesh: chan: 8 (over z, core), filt: 4 (over y, x).
Axes of the slice: x: 2, y: 2, z: 4, core: 2. Of those that a mesh axis runs over, the one named last changes fastest.
Arguments:
- inputs: bfloat16 [1024, 8, 1024], P('chan', 'filt'), may hold values from -6 to 6
- conv_kernel: bfloat16 [27, 1024, 128], P(None, 'chan'), may hold values from -0.109375 to 0.109375
- proj_weight: bfloat16 [1024, 1024], P('filt', 'chan'), may hold values from -0.25 to 0.25
- out_grad: bfloat16 [1024, 8, 1024], P('chan', 'filt'), may hold values from -6 to 6
Outputs:
- projected: bfloat16 [1024, 8, 1024], P('chan', 'filt')
- input_grad: bfloat16 [1024, 8, 1024], P('chan', 'filt')
- kernel_grad: float32 [27, 1024, 128], P(None, 'chan')
- weight_grad: float32 [1024, 1024], P('filt', 'chan')
The draws below stay inside these ranges and needn't reach their ends.
All inputs are finite; a program needn't handle non-finite values.
Results may differ from the reference program's by a relative error of at most 0.018.
Values may be sent and summed in bfloat16 or wider, within the bound.
No kernel may reach another device: no remote copies, remote signals or barrier semaphores. Data moves between devices by JAX's collectives and lax.ppermute only.
A program may use at most 128 MiB of HBM per device.

```python
import jax
import jax.numpy as jnp
from jax import lax

G = 128
NY = 32
NZ = 32
C = 1024
F = 1024
NX = 8
YZ = 1024


def spiked(entries, rng, source, target, blocks, factor):
    def block_of(axis_at):
        return (jnp.arange(entries.shape[axis_at]) // (entries.shape[axis_at] // blocks)).reshape((-1,) + (1,) * (entries.ndim - 1 - axis_at))

    first = jax.random.permutation(rng, blocks)[block_of(target)]
    far = (block_of(target) + blocks // 2) % blocks
    return jnp.where((block_of(source) == first) | (block_of(source) == far), factor * entries, entries)


def level_of(rng, shape, cuts, smallest, high):
    gain = 1.0
    for axis_at, shards_of in cuts:
        draws = jax.random.uniform(jax.random.fold_in(jax.random.fold_in(rng, 6), axis_at), (shards_of,), jnp.float32, smallest / len(cuts), high / len(cuts))
        gain = gain * jnp.repeat(jnp.exp(draws), shape[axis_at] // shards_of).reshape((-1,) + (1,) * (len(shape) - 1 - axis_at))
    return gain


def gaussian(rng, dims, scale, most, pieces=(), held_as=jnp.bfloat16):
    loudness = level_of(rng, dims, pieces, -0.22, 0.18) if pieces else 1.0
    values = jax.random.normal(rng, dims, jnp.float32) * scale * loudness
    return jnp.minimum(jnp.maximum(values, -most), most).astype(held_as)


def gaussian_with(own_key, dims, deviation, reach, cuts, heavy, dtype=jnp.bfloat16):
    drawn = deviation * jax.random.normal(own_key, dims, jnp.float32)
    if cuts:
        drawn = drawn * level_of(own_key, dims, cuts, -0.22, 0.18)
    return jnp.clip(spiked(drawn, jax.random.fold_in(own_key, 3), *heavy), -reach, reach).astype(dtype)


def setup_inputs(seed: int = 0) -> dict:
    keys = jax.random.split(jax.random.key(seed), 5)
    inputs = gaussian(keys[0], (C, NX, YZ), 1.0, 6.0, ((0, 8), (1, 4)))
    conv_kernel = gaussian(keys[1], (27, C, G), (27 * G) ** -0.5, 0.109375, ((1, 8),))
    proj_weight = gaussian_with(keys[2], (F, C), C ** -0.5, 0.25, ((0, 4), (1, 8)), (1, 0, 8, 2.0))
    out_grad = gaussian(keys[3], (F, NX, YZ), 1.0, 6.0, ((0, 8), (1, 4)))
    return {"inputs": inputs, "conv_kernel": conv_kernel, "proj_weight": proj_weight, "out_grad": out_grad}


def activation(values):
    return jax.nn.gelu(values, approximate=True)


def tap_list():
    result = []
    for shift_a in (-1, 0, 1):
        for shift_b in (-1, 0, 1):
            for shift_c in (-1, 0, 1):
                result.append((shift_a, shift_b, shift_c))
    return result


def reference(inputs, conv_kernel, proj_weight, out_grad):
    groups = C // G
    volume = inputs.astype(jnp.float32).reshape(C, NX, NY, NZ)
    padded = jnp.pad(volume, ((0, 0), (1, 1), (1, 1), (1, 1)))
    pre = jnp.zeros((groups, G, NX * NY * NZ), jnp.float32)
    for tap, (shift_a, shift_b, shift_c) in enumerate(tap_list()):
        window = padded[:, 1 + shift_a:1 + shift_a + NX, 1 + shift_b:1 + shift_b + NY, 1 + shift_c:1 + shift_c + NZ].reshape(groups, G, -1)
        kernel_tap = conv_kernel[tap].astype(jnp.float32).reshape(groups, G, G)
        pre = pre + jnp.einsum('gok,gkn->gon', kernel_tap, window)
    pre = pre.reshape(C, -1)
    hidden = activation(pre).astype(jnp.bfloat16)
    projected = jnp.zeros((F, NX * NY * NZ), jnp.float32)
    for group in range(groups):
        term = jnp.dot(proj_weight[:, group * G:(group + 1) * G], hidden[group * G:(group + 1) * G], preferred_element_type=jnp.float32)
        rounded = lax.optimization_barrier(term.astype(jnp.bfloat16))
        projected = projected + rounded.astype(jnp.float32)
    projected = projected.astype(jnp.bfloat16)
    grad_flat = out_grad.reshape(F, -1)
    hidden_grad = jnp.dot(proj_weight.T, grad_flat, preferred_element_type=jnp.float32)
    weight_grad = jnp.dot(grad_flat, hidden.T, preferred_element_type=jnp.float32)
    derivative = jax.jvp(activation, (pre,), (jnp.ones_like(pre),))[1]
    conv_grad = (hidden_grad * derivative).astype(jnp.bfloat16)
    grad_float = conv_grad.astype(jnp.float32)
    grad_pad = jnp.pad(grad_float.reshape(C, NX, NY, NZ), ((0, 0), (1, 1), (1, 1), (1, 1)))
    grad_groups = grad_float.reshape(groups, G, -1)
    input_grad = jnp.zeros((groups, G, NX * NY * NZ), jnp.float32)
    kernel_parts = []
    for tap, (shift_a, shift_b, shift_c) in enumerate(tap_list()):
        kernel_tap = conv_kernel[tap].astype(jnp.float32).reshape(groups, G, G)
        moved = grad_pad[:, 1 - shift_a:1 - shift_a + NX, 1 - shift_b:1 - shift_b + NY, 1 - shift_c:1 - shift_c + NZ].reshape(groups, G, -1)
        input_grad = input_grad + jnp.einsum('gok,gon->gkn', kernel_tap, moved)
        window = padded[:, 1 + shift_a:1 + shift_a + NX, 1 + shift_b:1 + shift_b + NY, 1 + shift_c:1 + shift_c + NZ].reshape(groups, G, -1)
        kernel_parts.append(jnp.einsum('gon,gkn->gok', grad_groups, window).reshape(C, G))
    kernel_grad = jnp.stack(kernel_parts, axis=0)
    input_grad = input_grad.reshape(C, NX, NY * NZ).astype(jnp.bfloat16)
    return projected.reshape(F, NX, NY * NZ), input_grad, kernel_grad, weight_grad
```

```python
import functools

import jax
import jax.numpy as jnp
from jax import lax
from jax.experimental import pallas as pl
from jax.experimental.pallas import tpu as pltpu
from jax.sharding import PartitionSpec as P

NY = 32
NZ = 32
TAPS = [(a, b, c) for a in (-1, 0, 1) for b in (-1, 0, 1) for c in (-1, 0, 1)]
BF16 = jnp.bfloat16
F32 = jnp.float32
VMEM = pl.BlockSpec(memory_space=pltpu.VMEM)
SMEM = pl.BlockSpec(memory_space=pltpu.SMEM)
ANY = pl.BlockSpec(memory_space=pl.ANY)
LIMIT = 40 << 20


def cost(flops, moved):
    return pl.CostEstimate(flops=flops, bytes_accessed=moved, transcendentals=0)


def neighbours(array, axis):
    size = lax.axis_size(axis)
    up = [(i, i + 1) for i in range(size - 1)]
    down = [(j, i) for i, j in up]
    before = lax.ppermute(array[-1:], axis, up)
    after = lax.ppermute(array[:1], axis, down)
    return before, after


def swap_cores(block):
    size = lax.axis_size("chan")
    return lax.ppermute(block, "chan", [(i, i ^ 1) for i in range(size)])


def hop(block, step, first, last):
    pairs = []
    for position in range(first, last + 1):
        for core in (0, 1):
            pairs.append((2 * position + core, 2 * (position + step) + core))
    return lax.ppermute(block, "chan", pairs)


def line_gather(block):
    positions = lax.axis_size("chan") // 2
    entries = [(0, block, swap_cores(block))]
    below = above = block
    for distance in range(1, positions):
        below = hop(below, 1, distance - 1, positions - 2)
        above = hop(above, -1, 1, positions - distance)
        entries.append((-distance, below, swap_cores(below)))
        entries.append((distance, above, swap_cores(above)))
    return entries


def shifted(plane, step):
    wide = plane.astype(F32)
    rolled = pltpu.roll(wide, (-step) % wide.shape[0], axis=0)
    place = lax.broadcasted_iota(jnp.int32, wide.shape, 0) % NZ
    edge = NZ - 1 if step > 0 else 0
    return jnp.where(place == edge, 0.0, rolled).astype(BF16)


def fill_plane(scratch, index, plane):
    cells, width = plane.shape
    pad = jnp.zeros((NZ, width), BF16)
    for slot, step in enumerate((-1, 0, 1)):
        scratch[slot, index, 0:NZ] = pad
        scratch[slot, index, NZ + cells : NZ + cells + NZ] = pad
        scratch[slot, index, NZ : NZ + cells] = plane if step == 0 else shifted(plane, step)


def fill(scratch, main_ref, before_ref, after_ref):
    planes = main_ref.shape[0]
    fill_plane(scratch, 0, before_ref[0])
    for index in range(planes):
        fill_plane(scratch, index + 1, main_ref[index])
    fill_plane(scratch, planes + 1, after_ref[0])


def padded(planes, cells, width):
    return pltpu.VMEM((3, planes + 2, cells + 2 * NZ, width), BF16)


def gelu_pair(v):
    k = 0.7978845608028654
    t = jnp.tanh(k * (v + 0.044715 * (v * v * v)))
    half = 0.5 * (1.0 + t)
    derivative = half + 0.5 * v * (1.0 - t * t) * (k * (1.0 + 3 * 0.044715 * (v * v)))
    return v * half, derivative


def forward_body(x_ref, before_ref, after_ref, k_ref, hidden_ref, slope_ref, scratch, flat, *, rows):
    planes, cells, width = x_ref.shape
    fill(scratch, x_ref, before_ref, after_ref)
    for tap in range(len(TAPS)):
        flat[:, tap * width : (tap + 1) * width] = k_ref[tap]
    per_plane = cells // rows

    def step(i, carry):
        plane = i // per_plane
        start = (i % per_plane) * rows
        parts = []
        for a, b, c in TAPS:
            at = pl.ds(pl.multiple_of(start + NZ + NZ * b, NZ), rows)
            parts.append(scratch[c + 1, plane + 1 + a, at, :])
        pre = lax.dot_general(
            jnp.concatenate(parts, axis=1),
            flat[...],
            (((1,), (1,)), ((), ())),
            preferred_element_type=F32,
        )
        hidden, slope = gelu_pair(pre)
        out = pl.ds(pl.multiple_of(i * rows, rows), rows)
        hidden_ref[out, :] = hidden.astype(BF16)
        slope_ref[out, :] = slope
        return carry

    lax.fori_loop(0, planes * per_plane, step, 0)


def forward(x, before, after, kernel):
    planes, cells, width = x.shape
    count = planes * cells
    return pl.pallas_call(
        functools.partial(forward_body, rows=1024),
        out_shape=(
            jax.ShapeDtypeStruct((count, width), BF16),
            jax.ShapeDtypeStruct((count, width), F32),
        ),
        in_specs=[VMEM] * 4,
        out_specs=(VMEM, VMEM),
        scratch_shapes=[padded(planes, cells, width), pltpu.VMEM((width, 27 * width), BF16)],
        compiler_params=pltpu.CompilerParams(vmem_limit_bytes=LIMIT),
        cost_estimate=cost(54 * count * width * width, 8 * count * width),
        name="conv_forward",
    )(x, before, after, kernel)


def collect(position, blocks, buffer, sems, distances):
    own_core = position[1]
    limit = buffer.shape[0]

    def each(action):
        for entry, distance in enumerate(distances):
            at = position[0] + distance

            @pl.when(jnp.logical_and(at >= 0, at < limit))
            def _():
                for side in (0, 1):
                    core = own_core if side == 0 else 1 - own_core
                    action(
                        pltpu.make_async_copy(
                            blocks[2 * entry + side],
                            buffer.at[at, core],
                            sems.at[2 * entry + side],
                        )
                    )

    each(lambda copy: copy.start())
    each(lambda copy: copy.wait())


def all_columns(buffer, rows):
    parts = []
    for position in range(buffer.shape[0]):
        for core in (0, 1):
            parts.append(buffer[position, core, rows, :])
    return jnp.concatenate(parts, axis=1)


def hidden_grad_body(position_ref, w_ref, slope_ref, hidden_ref, *rest, distances, rows):
    blocks = rest[: 2 * len(distances)]
    cg_ref, wg_ref, buffer, turned, sems = rest[2 * len(distances) :]
    position = (position_ref[0], position_ref[1])
    collect(position, blocks, buffer, sems, distances)
    count = slope_ref.shape[0]

    def step(i, carry):
        at = pl.ds(pl.multiple_of(i * rows, rows), rows)
        grad = jnp.dot(all_columns(buffer, at), w_ref[...], preferred_element_type=F32)
        cg_ref[at, :] = (grad * slope_ref[at, :]).astype(BF16)
        return carry

    lax.fori_loop(0, count // rows, step, 0)
    turned[...] = hidden_ref[...].T
    width = turned.shape[0]
    for chip in range(buffer.shape[0]):
        both = jnp.concatenate([buffer[chip, 0], buffer[chip, 1]], axis=1)
        part = jnp.dot(turned[...], both, preferred_element_type=F32).astype(BF16)
        wg_ref[2 * chip] = part[:, :width]
        wg_ref[2 * chip + 1] = part[:, width:]


def hidden_grad(position, w_cols, slope, hidden, entries):
    count, width = hidden.shape
    filters = w_cols.shape[0]
    distances = [entry[0] for entry in entries]
    blocks = [block for entry in entries for block in entry[1:]]
    return pl.pallas_call(
        functools.partial(hidden_grad_body, distances=distances, rows=512),
        out_shape=(
            jax.ShapeDtypeStruct((count, width), BF16),
            jax.ShapeDtypeStruct((filters // width, width, width), BF16),
        ),
        in_specs=[SMEM, VMEM, VMEM, VMEM] + [ANY] * len(blocks),
        out_specs=(VMEM, VMEM),
        scratch_shapes=[
            pltpu.VMEM((filters // width // 2, 2, count, width), BF16),
            pltpu.VMEM((width, count), BF16),
            pltpu.SemaphoreType.DMA((len(blocks),)),
        ],
        compiler_params=pltpu.CompilerParams(vmem_limit_bytes=LIMIT),
        cost_estimate=cost(4 * count * width * filters, 2 * count * filters),
        name="hidden_grad",
    )(position, w_cols, slope, hidden, *blocks)


def project_body(position_ref, w_ref, *rest, distances, rows):
    blocks = rest[: 2 * len(distances)]
    out_ref, buffer, sems = rest[2 * len(distances) :]
    collect((position_ref[0], position_ref[1]), blocks, buffer, sems, distances)

    def step(i, carry):
        at = pl.ds(pl.multiple_of(i * rows, rows), rows)
        out_ref[at, :] = lax.dot_general(
            all_columns(buffer, at),
            w_ref[...],
            (((1,), (1,)), ((), ())),
            preferred_element_type=F32,
        ).astype(BF16)
        return carry

    lax.fori_loop(0, out_ref.shape[0] // rows, step, 0)


def project(position, w_rows, entries):
    count = entries[0][1].shape[0]
    width, channels = w_rows.shape
    distances = [entry[0] for entry in entries]
    blocks = [block for entry in entries for block in entry[1:]]
    return pl.pallas_call(
        functools.partial(project_body, distances=distances, rows=512),
        out_shape=jax.ShapeDtypeStruct((count, width), BF16),
        in_specs=[SMEM, VMEM] + [ANY] * len(blocks),
        out_specs=VMEM,
        scratch_shapes=[
            pltpu.VMEM((channels // width // 2, 2, count, width), BF16),
            pltpu.SemaphoreType.DMA((len(blocks),)),
        ],
        compiler_params=pltpu.CompilerParams(vmem_limit_bytes=LIMIT),
        cost_estimate=cost(2 * count * width * channels, 2 * count * channels),
        name="project",
    )(position, w_rows, *blocks)


def kernel_grad_body(x_ref, before_ref, after_ref, cg_ref, out_ref, scratch, turned):
    planes, cells, width = x_ref.shape
    fill(scratch, x_ref, before_ref, after_ref)
    turned[...] = cg_ref[...].T
    for a in (-1, 0, 1):
        for b in (-1, 0, 1):
            total = None
            for plane in range(planes):
                start = NZ + NZ * b
                parts = [scratch[c, plane + 1 + a, start : start + cells, :] for c in range(3)]
                part = jnp.dot(
                    turned[:, plane * cells : (plane + 1) * cells],
                    jnp.concatenate(parts, axis=1),
                    preferred_element_type=F32,
                )
                total = part if total is None else total + part
            tap = 9 * (a + 1) + 3 * (b + 1)
            for c in range(3):
                out_ref[tap + c] = total[:, c * width : (c + 1) * width].astype(BF16)


def kernel_grad_terms(x, before, after, conv_grad):
    planes, cells, width = x.shape
    count = planes * cells
    return pl.pallas_call(
        kernel_grad_body,
        out_shape=jax.ShapeDtypeStruct((27, width, width), BF16),
        in_specs=[VMEM] * 4,
        out_specs=VMEM,
        scratch_shapes=[padded(planes, cells, width), pltpu.VMEM((width, count), BF16)],
        compiler_params=pltpu.CompilerParams(vmem_limit_bytes=LIMIT),
        cost_estimate=cost(54 * count * width * width, 4 * count * width),
        name="kernel_grad",
    )(x, before, after, conv_grad)


def input_grad_body(cg_ref, before_ref, after_ref, k_ref, out_ref, scratch, *, rows):
    planes, cells, width = cg_ref.shape
    fill(scratch, cg_ref, before_ref, after_ref)
    per_plane = cells // rows

    def step(i, carry):
        plane = i // per_plane
        start = (i % per_plane) * rows
        parts = []
        for a, b, c in TAPS:
            at = pl.ds(pl.multiple_of(start + NZ - NZ * b, NZ), rows)
            parts.append(scratch[1 - c, plane + 1 - a, at, :])
        grad = jnp.dot(jnp.concatenate(parts, axis=1), k_ref[...], preferred_element_type=F32)
        out_ref[pl.ds(pl.multiple_of(i * rows, rows), rows), :] = grad.astype(BF16)
        return carry

    lax.fori_loop(0, planes * per_plane, step, 0)


def input_grad_of(conv_grad, before, after, kernel):
    planes, cells, width = conv_grad.shape
    count = planes * cells
    return pl.pallas_call(
        functools.partial(input_grad_body, rows=1024),
        out_shape=jax.ShapeDtypeStruct((count, width), BF16),
        in_specs=[VMEM] * 4,
        out_specs=VMEM,
        scratch_shapes=[padded(planes, cells, width)],
        compiler_params=pltpu.CompilerParams(vmem_limit_bytes=LIMIT),
        cost_estimate=cost(54 * count * width * width, 4 * count * width),
        name="input_grad",
    )(conv_grad, before, after, kernel.reshape(27 * width, width))


def sum_body(*refs):
    shares = refs[:-2]
    kernel_ref, weight_ref = refs[-2:]
    total = shares[0][...].astype(F32)
    for share in shares[1:]:
        total = total + share[...].astype(F32)
    rows, width = kernel_ref.shape
    kernel_ref[...] = total[:rows].astype(BF16)
    for at in range(0, weight_ref.shape[0], width):
        weight_ref[at : at + width, :] = total[rows + at : rows + at + width].T


def sum_shares(shares, kernel_rows):
    rows, width = shares[0].shape
    return pl.pallas_call(
        sum_body,
        out_shape=(
            jax.ShapeDtypeStruct((kernel_rows, width), BF16),
            jax.ShapeDtypeStruct((rows - kernel_rows, width), F32),
        ),
        in_specs=[VMEM] * len(shares),
        out_specs=(VMEM, VMEM),
        cost_estimate=cost(rows * width * len(shares), 2 * rows * width * len(shares)),
        name="sum_shares",
    )(*shares)


def place_body(me_ref, *refs):
    shares, out_ref = (refs[:-1], refs[-1])
    for mask, share in enumerate(shares):
        out_ref[me_ref[0] ^ mask] = share[...].astype(F32)


def place_shares(me, shares):
    rows, width = shares[0].shape
    return pl.pallas_call(
        place_body,
        out_shape=jax.ShapeDtypeStruct((len(shares), rows, width), F32),
        in_specs=[SMEM] + [VMEM] * len(shares),
        out_specs=VMEM,
        cost_estimate=cost(rows * width, 6 * rows * width * len(shares)),
        name="place_shares",
    )(me, *shares)


def body(inputs, conv_kernel, proj_weight, out_grad):
    width, planes, cells = inputs.shape
    count = planes * cells
    chan = lax.axis_index("chan")
    filt = lax.axis_index("filt")
    parts = lax.axis_size("filt")
    position = jnp.stack([chan // 2, chan % 2]).astype(jnp.int32)

    grad_cells = jnp.transpose(out_grad, (1, 2, 0)).reshape(count, width)
    grad_entries = line_gather(grad_cells)

    x = jnp.transpose(inputs, (1, 2, 0))
    x_before, x_after = neighbours(x, "filt")
    w_cols = lax.all_gather(proj_weight, "filt", axis=0, tiled=True)
    w_rows = lax.all_to_all(w_cols, "chan", split_axis=0, concat_axis=1, tiled=True)

    hidden, slope = forward(x, x_before, x_after, conv_kernel)

    conv_grad, weight_terms = hidden_grad(position, w_cols, slope, hidden, grad_entries)

    hidden_sent, _ = lax.optimization_barrier((hidden, grad_entries[-1][2]))
    hidden_entries = line_gather(hidden_sent)

    conv_grad = conv_grad.reshape(planes, cells, width)
    g_before, g_after = neighbours(conv_grad, "filt")
    terms = kernel_grad_terms(x, x_before, x_after, conv_grad.reshape(count, width))

    kernel_rows = 27 * width // parts
    terms = terms.reshape(parts, kernel_rows, width)
    weight_terms = weight_terms.reshape(parts, -1, width)
    shares = []
    for mask in range(parts):
        to = filt ^ mask
        share = jnp.concatenate(
            [
                lax.dynamic_index_in_dim(terms, to, 0, keepdims=False),
                lax.dynamic_index_in_dim(weight_terms, to, 0, keepdims=False),
            ],
            axis=0,
        )
        if mask:
            share = lax.ppermute(share, "filt", [(i, i ^ mask) for i in range(parts)])
        shares.append(share)

    input_grad = input_grad_of(conv_grad, g_before, g_after, conv_kernel)
    input_grad = jnp.transpose(input_grad.reshape(planes, cells, width), (2, 0, 1))

    kernel_share, weight_grad = sum_shares(shares, kernel_rows)
    pieces = [kernel_share]
    for mask in range(1, parts):
        pieces.append(lax.ppermute(kernel_share, "filt", [(i, i ^ mask) for i in range(parts)]))
    kernel_grad = place_shares(filt.astype(jnp.int32).reshape(1), pieces)
    kernel_grad = kernel_grad.reshape(27, width, width)

    projected = project(position, w_rows, hidden_entries)
    projected = jnp.transpose(projected.reshape(planes, cells, width), (2, 0, 1))
    return (projected, input_grad, kernel_grad, weight_grad)


def solution(mesh):
    in_specs = (
        P("chan", "filt", None),
        P(None, "chan", None),
        P("filt", "chan"),
        P("chan", "filt", None),
    )
    out_specs = (
        P("chan", "filt", None),
        P("chan", "filt", None),
        P(None, "chan", None),
        P("filt", "chan"),
    )
    return jax.shard_map(body, mesh=mesh, in_specs=in_specs, out_specs=out_specs, check_vma=False)
```
